128 devices in a mesh: seq: 16 (over x, y), head: 8 (over z, core).
Axes of the slice: x: 4, y: 4, z: 4, core: 2. Of those that a mesh axis runs over, the one named last changes fastest.
Arguments:
- hidden_in: bfloat16 [16384, 2048], P('seq', 'head'), may hold values from -9 to 9
- w_query: bfloat16 [2048, 2048], P(None, 'head'), may hold values from -0.125 to 0.125
- w_key: bfloat16 [2048, 2048], P(None, 'head'), may hold values from -0.125 to 0.125
- w_value: bfloat16 [2048, 4096], P(None, 'head'), may hold values from -0.125 to 0.125
- w_gate: bfloat16 [2048, 4096], P(None, 'head'), may hold values from -0.125 to 0.125
- w_beta: bfloat16 [2048, 32], P(None, 'head'), may hold values from -0.8 to 0.8
- w_alpha: bfloat16 [2048, 32], P(None, 'head'), may hold values from -0.125 to 0.125
- dt_bias: float32 [32], P('head'), may hold values from -1 to 1
- head_decay: float32 [32], P('head'), may hold values from 6.1035156e-06 to 0.05
- conv_query: bfloat16 [4, 2048], P(None, 'head'), may hold values from -3 to 3
- conv_key: bfloat16 [4, 2048], P(None, 'head'), may hold values from -3 to 3
- conv_value: bfloat16 [4, 4096], P(None, 'head'), may hold values from -3 to 3
- norm_weight: float32 [128], replicated, may hold values from 0.25 to 1.75
- w_out: bfloat16 [4096, 2048], P('head'), may hold values from -0.09375 to 0.09375
- prompt_lengths: int32 [6], replicated, may hold values from 1 to 8192, 16384 in all
Outputs:
- layer_out: bfloat16 [16384, 2048], P('seq', 'head')
The draws below stay inside these ranges and needn't reach their ends.
Inputs may be any that keep to these rules, and one draw needn't show every extreme that they name: `prompt_lengths`: the lengths sum to 16384; the longest is 8192.
All inputs are finite; a program needn't handle non-finite values.
Results may differ from the reference program's by a relative error of at most 0.018.
Values may be sent and summed in bfloat16 or wider, within the bound.
A program may use at most 128 MiB of HBM per device.

```python
import math
import jax
import jax.numpy as jnp
import numpy as np
from jax import lax

D = 2048
KHEADS = 16
VHEADS = 32
HEAD_DIM = 128
CONV = 4
BLOCK = 64
PROMPTS = 6
TOKENS = 16384
MOST = 8192
N_HEAD = 8


def draw_head_decay(key, part):
    pick_key, slow_key, fast_key = jax.random.split(key, 3)
    slow_share = 0.5
    slow_rate = jnp.exp(jax.random.uniform(slow_key, (VHEADS,), jnp.float32, math.log(0.1 / TOKENS), math.log(1.0 / TOKENS)))
    fast_rate = jnp.exp(jax.random.uniform(fast_key, (VHEADS,), jnp.float32, math.log(0.005), math.log(0.05)))
    chosen = jax.random.uniform(pick_key, (VHEADS,), jnp.float32) < slow_share
    return jnp.where(chosen, slow_rate, fast_rate).astype(jnp.float32)


def strong_channel(key):
    return jax.random.randint(jax.random.fold_in(key, 11), (), 0, D)


def draw_hidden_in(key, part):
    noise_key, level_key = jax.random.split(jax.random.fold_in(key, 23), 2)
    noise = jnp.clip(jax.random.normal(noise_key, (TOKENS, D), jnp.float32), -6.0, 6.0)
    level = jax.random.uniform(level_key, (TOKENS, 1), jnp.float32, 6.0, 9.0)
    column = jnp.arange(D)[None, :] == strong_channel(key)
    return jnp.where(column, level, noise).astype(jnp.bfloat16)


def draw_w_beta(key, part):
    noise_key, row_key = jax.random.split(jax.random.fold_in(key, 37), 2)
    noise = jnp.clip(jax.random.normal(noise_key, (D, VHEADS), jnp.float32), -6.0, 6.0) * D ** (-0.5)
    strong_row = jax.random.uniform(row_key, (1, VHEADS), jnp.float32, -0.78, -0.6)
    column = jnp.arange(D)[:, None] == strong_channel(key)
    return jnp.where(column, strong_row, noise).astype(jnp.bfloat16)


def level_of(own_key, dims, cuts, low, largest):
    def one(dim, blocks):
        steps = jax.random.uniform(jax.random.fold_in(jax.random.fold_in(own_key, 6), dim), (blocks,), jnp.float32, low / len(cuts), largest / len(cuts))
        return jnp.repeat(jnp.exp(steps), dims[dim] // blocks).reshape((-1,) + (1,) * (len(dims) - dim - 1))

    factor_of = one(*cuts[0])
    for cut in cuts[1:]:
        factor_of = factor_of * one(*cut)
    return factor_of


def profile(number_of, total, most, skew):
    weights = [(1 << 20) // math.isqrt(rank ** skew) + 1 for rank in range(2, number_of + 1)]
    surplus, given = total - most - (number_of - 1), [1] * (number_of - 1)
    while surplus > 0:
        movable = [i for i in range(number_of - 1) if given[i] < most]
        pool, budget = sum([weights[i] for i in movable]), surplus
        for i in movable:
            addition = min(most - given[i], max(1, budget * weights[i] // pool), surplus)
            given[i] = given[i] + addition
            surplus = surplus - addition
    return np.array([most] + given)


def ragged(own_key, number_of, total, most, lean):
    if number_of == 2:
        one = jax.random.randint(own_key, (), max(1, total - most), min(most, total - 1) + 1)
        return jnp.stack([one, total - one])
    tallies = jnp.asarray(profile(number_of, total, most, lean), jnp.int32)
    pairs = (number_of - 1) // 2
    donor, receiver = tallies[1:1 + 2 * pairs:2], tallies[2:2 + 2 * pairs:2]
    slack = jnp.minimum(donor - 1, most - receiver)
    moved = jax.random.randint(jax.random.fold_in(own_key, 1), (pairs,), 0, 1 << 20) % (slack + 1)
    tallies = tallies.at[1:1 + 2 * pairs:2].set(donor - moved).at[2:2 + 2 * pairs:2].set(receiver + moved)
    return tallies[jax.random.permutation(jax.random.fold_in(own_key, 2), number_of)]


def gaussian(key, extent, deviation, most, cuts=(), held_as=jnp.bfloat16):
    values = jax.random.normal(key, extent, jnp.float32) * deviation
    if len(cuts) > 0:
        values = level_of(key, extent, cuts, -0.22, 0.18) * values
    return jnp.clip(values, min=-most, max=most).astype(held_as)


def setup_inputs(seed: int = 0) -> dict:
    keys = jax.random.split(jax.random.key(seed), 16)
    return {
        "hidden_in": draw_hidden_in(jax.random.fold_in(keys[15], 71), 0),
        "w_query": gaussian(keys[1], (D, KHEADS * HEAD_DIM), D ** -0.5, 0.125, ((1, 8),)),
        "w_key": gaussian(keys[2], (D, KHEADS * HEAD_DIM), D ** -0.5, 0.125, ((1, 8),)),
        "w_value": gaussian(keys[3], (D, VHEADS * HEAD_DIM), D ** -0.5, 0.125, ((1, 8),)),
        "w_gate": gaussian(keys[4], (D, VHEADS * HEAD_DIM), D ** -0.5, 0.125, ((1, 8),)),
        "w_beta": draw_w_beta(jax.random.fold_in(keys[15], 71), 0),
        "w_alpha": gaussian(keys[6], (D, VHEADS), D ** -0.5, 0.125, ((1, 8),)),
        "dt_bias": jnp.clip(jax.random.uniform(keys[7], (VHEADS,), jnp.float32, -1.0, 1.0) * level_of(keys[7], (VHEADS,), ((0, 8),), -0.4, 0.0), -1.0, 1.0),
        "head_decay": draw_head_decay(jax.random.fold_in(keys[15], 71), 0),
        "conv_query": gaussian(keys[9], (CONV, KHEADS * HEAD_DIM), CONV ** -0.5, 3.0, ((1, 8),)),
        "conv_key": gaussian(keys[10], (CONV, KHEADS * HEAD_DIM), CONV ** -0.5, 3.0, ((1, 8),)),
        "conv_value": gaussian(keys[11], (CONV, VHEADS * HEAD_DIM), CONV ** -0.5, 3.0, ((1, 8),)),
        "norm_weight": jnp.clip(1.0 + 0.15 * jax.random.normal(keys[12], (HEAD_DIM,), jnp.float32), 0.25, 1.75),
        "w_out": gaussian(keys[13], (VHEADS * HEAD_DIM, D), (VHEADS * HEAD_DIM) ** -0.5, 0.09375, ((0, 8),)),
        "prompt_lengths": ragged(keys[14], PROMPTS, TOKENS, MOST, 2).astype(jnp.int32),
    }


highest = lax.Precision.HIGHEST

def composed_product(form, left_side, right_side):
    return jnp.einsum(form, left_side, right_side, precision=highest)

def unit_scale(values_in):
    return values_in * lax.rsqrt(lax.optimization_barrier(jnp.sum(values_in * values_in, axis=-1, keepdims=True)) + 1e-06)

def block_terms(queries, keys_in, values_in, betas, log_decay, resets):
    width_in = queries.shape[1]
    segment = jnp.cumsum(resets)
    cumulative = jnp.cumsum(log_decay, axis=1)
    spread = cumulative[:, :, None] - cumulative[:, None, :]
    position = jnp.arange(width_in)
    causal = position[:, None] >= position[None, :]
    strictly = position[:, None] > position[None, :]
    joined = segment[:, None] == segment[None, :]
    factor = jnp.where((causal & joined)[None], jnp.exp(jnp.minimum(spread, 0.0)), 0.0)
    scaled = jnp.where(segment[None, :] == 0, jnp.exp(cumulative), 0.0)
    similar = composed_product('hik,hjk->hij', keys_in, keys_in)
    system = jnp.eye(width_in, dtype=queries.dtype)[None] + betas[:, :, None] * jnp.where(strictly[None], factor * similar, 0.0)
    right_hand = jnp.concatenate([betas[:, :, None] * values_in, (betas * scaled)[:, :, None] * keys_in], axis=-1)
    solved = jax.scipy.linalg.solve_triangular(system, right_hand, lower=True, unit_diagonal=True)
    value_width = values_in.shape[-1]
    corrected_values = solved[..., :value_width]
    w_keys = solved[..., value_width:]
    attend = factor * composed_product('hik,hjk->hij', queries, keys_in)
    trailing_keys = factor[:, -1, :, None] * keys_in
    identity_k = jnp.eye(keys_in.shape[-1], dtype=queries.dtype)
    state_transfer = scaled[:, -1, None, None] * identity_k[None] - composed_product('hck,hcl->hkl', trailing_keys, w_keys)
    inserted_values = composed_product('iws,iwe->ise', trailing_keys, corrected_values)
    producer_fn = scaled[:, :, None] * queries - composed_product('hij,hjk->hik', attend, w_keys)
    self_output = composed_product('hij,hjv->hiv', attend, corrected_values)
    return (producer_fn, self_output, state_transfer, inserted_values)

def prompt_starts(lengths_in, positions):
    offsets = jnp.cumsum(lengths_in) - lengths_in
    starts = lax.optimization_barrier(jnp.max(jnp.where(offsets[None, :] <= positions[:, None], offsets[None, :], 0), axis=1))
    return (starts, (positions == starts).astype(jnp.float32))

def short_conv(raw_in, prefix_rows, taps, positions, starts):
    reach = taps.shape[0]
    row_count = raw_in.shape[0]
    extended = jnp.concatenate([prefix_rows, raw_in], axis=0).astype(jnp.float32)
    running = jnp.zeros(raw_in.shape, jnp.float32)
    for tap_index in range(reach):
        tap_lag = reach - 1 - tap_index
        inside = (positions - tap_lag >= starts).astype(jnp.float32)
        running = running + taps[tap_index].astype(jnp.float32)[None, :] * extended[tap_index:tap_index + row_count] * inside[:, None]
    return jax.nn.silu(running)

def to_blocks(array_in):
    row_count, head_count, width_in = array_in.shape
    return array_in.reshape(row_count // BLOCK, BLOCK, head_count, width_in).transpose(0, 2, 1, 3)

def to_blocks_flat(array_in):
    row_count, head_count = array_in.shape
    return array_in.reshape(row_count // BLOCK, BLOCK, head_count).transpose(0, 2, 1)

def reference(hidden_in, w_query, w_key, w_value, w_gate, w_beta, w_alpha, dt_bias, head_decay, conv_query, conv_key, conv_value, norm_weight, w_out, prompt_lengths):
    raw_q = jnp.dot(hidden_in.astype(jnp.float32), w_query.astype(jnp.float32), preferred_element_type=jnp.float32).astype(jnp.bfloat16)
    raw_k = jnp.dot(hidden_in.astype(jnp.float32), w_key.astype(jnp.float32), preferred_element_type=jnp.float32).astype(jnp.bfloat16)
    raw_v = jnp.dot(hidden_in.astype(jnp.float32), w_value.astype(jnp.float32), preferred_element_type=jnp.float32).astype(jnp.bfloat16)
    raw_z = jnp.dot(hidden_in.astype(jnp.float32), w_gate.astype(jnp.float32), preferred_element_type=jnp.float32).astype(jnp.bfloat16)
    betas = jax.nn.sigmoid(jnp.dot(hidden_in.astype(jnp.float32), w_beta.astype(jnp.float32), preferred_element_type=jnp.float32))
    log_decay = -head_decay[None, :] * jax.nn.softplus(jnp.dot(hidden_in.astype(jnp.float32), w_alpha.astype(jnp.float32), preferred_element_type=jnp.float32) + dt_bias[None, :])
    positions = jnp.arange(TOKENS, dtype=jnp.int32)
    starts, resets = prompt_starts(prompt_lengths, positions)
    conv_q = short_conv(raw_q, jnp.zeros((CONV - 1, raw_q.shape[1]), jnp.bfloat16), conv_query, positions, starts)
    conv_k = short_conv(raw_k, jnp.zeros((CONV - 1, raw_k.shape[1]), jnp.bfloat16), conv_key, positions, starts)
    conv_v = short_conv(raw_v, jnp.zeros((CONV - 1, raw_v.shape[1]), jnp.bfloat16), conv_value, positions, starts)
    group_ratio = VHEADS // KHEADS
    queries = jnp.repeat(unit_scale(conv_q.reshape(TOKENS, KHEADS, HEAD_DIM)), group_ratio, axis=1) * HEAD_DIM ** (-0.5)
    keys_all = jnp.repeat(unit_scale(conv_k.reshape(TOKENS, KHEADS, HEAD_DIM)), group_ratio, axis=1)
    values_all = conv_v.reshape(TOKENS, VHEADS, HEAD_DIM)
    blocks = (to_blocks(queries), to_blocks(keys_all), to_blocks(values_all), to_blocks_flat(betas), to_blocks_flat(log_decay), resets.reshape(TOKENS // BLOCK, BLOCK))

    def advance(passed_state, pieces):
        producer_fn, self_output, state_transfer, inserted_values = block_terms(*pieces)
        block_result = composed_product('upj,ujt->upt', producer_fn, passed_state) + self_output
        return (composed_product('ryp,rpj->ryj', state_transfer, passed_state) + inserted_values, block_result)
    _, block_results = lax.scan(advance, jnp.zeros((VHEADS, HEAD_DIM, HEAD_DIM), jnp.float32), blocks)
    attention_result = block_results.transpose(0, 2, 1, 3).reshape(TOKENS, VHEADS, HEAD_DIM)
    variance = lax.optimization_barrier(jnp.mean(attention_result * attention_result, axis=-1, keepdims=True))
    gate_vals = raw_z.astype(jnp.float32).reshape(TOKENS, VHEADS, HEAD_DIM)
    normed = (attention_result * lax.rsqrt(variance + 1e-06) * norm_weight[None, None, :] * jax.nn.silu(gate_vals)).astype(jnp.bfloat16)
    normed = normed.reshape(TOKENS, VHEADS * HEAD_DIM)
    group_width = VHEADS * HEAD_DIM // N_HEAD
    summed = jnp.zeros((TOKENS, D), jnp.float32)
    for group in range(N_HEAD):
        partial_sum = jnp.dot(normed[:, group * group_width:(group + 1) * group_width].astype(jnp.float32), w_out[group * group_width:(group + 1) * group_width].astype(jnp.float32), preferred_element_type=jnp.float32)
        rounded = lax.optimization_barrier(partial_sum.astype(jnp.bfloat16))
        summed = summed + rounded.astype(jnp.float32)
    return summed.astype(jnp.bfloat16)
```

```python
import functools
import jax
import jax.numpy as jnp
from jax import lax
from jax.experimental import pallas as pl
from jax.experimental.pallas import tpu as pltpu
BLOCK = 64
GROUP = 4
ROWS = BLOCK * GROUP
HD = 128
f32 = jnp.float32
bf16 = jnp.bfloat16

def dotf(a, b):
    return jnp.dot(a, b, preferred_element_type=f32)

def split2(x):
    hi = x.astype(bf16)
    return hi, (x - hi.astype(f32)).astype(bf16)

def sigmoid(x):
    return 1.0 / (1.0 + jnp.exp(-x))

def local_kernel(info, q_ref, k_ref, v_ref, halo_ref, ba_ref, dec_ref, taps_ref,
                 out_ref, lift_ref, st_ref, carry):
    step = pl.program_id(0)

    @pl.when(step == 0)
    def _():
        rows = lax.broadcasted_iota(jnp.int32, (HD, 2 * HD), 0)
        cols = lax.broadcasted_iota(jnp.int32, (HD, 2 * HD), 1)
        init = jnp.where(cols - HD == rows, 1.0, 0.0).astype(f32)
        for h in range(4):
            st_ref[h] = init
        carry[...] = halo_ref[...]

    base = info[0] + step * ROWS
    pos = base + lax.broadcasted_iota(jnp.int32, (ROWS, HD), 0)
    start = jnp.zeros((ROWS, HD), jnp.int32)
    off = info[1] * 0
    for n in range(6):
        start = jnp.maximum(start, jnp.where(pos >= off, off, 0))
        off = off + info[1 + n]
    rel = pos - start
    keep = [None, rel >= 1, rel >= 2, rel >= 3]

    def conv(ref, c, w):
        x0 = ref[:, c * HD:(c + 1) * HD].astype(f32)
        x = jnp.concatenate([carry[:, w * HD:(w + 1) * HD], x0], axis=0)
        carry[:, w * HD:(w + 1) * HD] = x0[ROWS - 8:]
        y = taps_ref[3:4, w * HD:(w + 1) * HD] * x0
        for lag in (1, 2, 3):
            t = taps_ref[3 - lag:4 - lag, w * HD:(w + 1) * HD]
            y = y + jnp.where(keep[lag], t * x[8 - lag:8 - lag + ROWS], 0.0)
        return y * sigmoid(y)

    def unit(x):
        return x * lax.rsqrt(jnp.sum(x * x, axis=-1, keepdims=True) + 1e-06)

    qs = [unit(conv(q_ref, c, c)) * HD ** (-0.5) for c in range(2)]
    ks = [unit(conv(k_ref, c, 2 + c)) for c in range(2)]
    vs = [conv(v_ref, c, 4 + c) for c in range(4)]
    qb = [x.astype(bf16) for x in qs]
    kb = [x.astype(bf16) for x in ks]
    ba = ba_ref[...]
    beta = sigmoid(ba)
    z = ba + dec_ref[0:1, :]
    g = dec_ref[1:2, :] * (jnp.maximum(z, 0.0) + jnp.log1p(jnp.exp(-jnp.abs(z))))

    ii = lax.broadcasted_iota(jnp.int32, (BLOCK, 256), 0)
    ll = lax.broadcasted_iota(jnp.int32, (BLOCK, 256), 1)
    jl = ll & (BLOCK - 1)
    xor = ii ^ jl
    head_of = ll >> 6
    low = lax.broadcasted_iota(jnp.int32, (BLOCK, HD), 1) < BLOCK
    ltri = jnp.where(
        lax.broadcasted_iota(jnp.int32, (BLOCK, BLOCK), 0)
        >= lax.broadcasted_iota(jnp.int32, (BLOCK, BLOCK), 1), 1.0, 0.0).astype(f32)
    hmask = [head_of == r for r in range(4)]

    def bd(m):
        z = jnp.zeros_like(m)
        return jnp.concatenate([jnp.where(hmask[r], m, z) for r in range(4)], axis=0)

    def packed(x, first, r):
        cols = [x[r, first + h:first + h + 1] for h in range(4)]
        return jnp.concatenate(
            [jnp.where(low, cols[0], cols[1]), jnp.where(low, cols[2], cols[3])], axis=1)

    def bdh(m):
        return bd(m).astype(bf16)

    def mul3(x, m):
        xh, xl = split2(x)
        mh = m.astype(bf16).astype(f32)
        ml = m - mh
        y = dotf(jnp.concatenate([xh, xl], axis=0), bdh(mh))
        return y[:BLOCK] + y[BLOCK:] + dotf(xh, bdh(ml))

    def mul1(x, m):
        return dotf(x.astype(bf16), bdh(m))

    blocks = range(GROUP)
    rs = [slice(b * BLOCK, (b + 1) * BLOCK) for b in blocks]
    L, A, spreads = [], [], []
    for b in blocks:
        r = rs[b]
        gm = jnp.where(ii > jl, packed(g, 4, r), 0.0)
        spread = jnp.dot(ltri, gm, precision=lax.Precision.HIGHEST, preferred_element_type=f32)
        spreads.append(spread)
        st2 = jnp.concatenate([start[r], start[r]], axis=1)
        mask = (ii >= jl) & (base + b * BLOCK + jl >= st2)
        factor = jnp.where(mask, jnp.exp(jnp.minimum(spread, 0.0)), 0.0)
        gr = []
        for c in range(2):
            kk = kb[c][r]
            gr.append(lax.dot_general(
                jnp.concatenate([kk, qb[c][r]], axis=0), jnp.concatenate([kk, kk], axis=0),
                (((1,), (1,)), ((), ())), preferred_element_type=f32))
        both = jnp.concatenate(gr, axis=1)
        L.append(jnp.where(ii > jl, packed(beta, 0, r) * factor * both[:BLOCK], 0.0))
        A.append(factor * both[BLOCK:])
    eye = jnp.where(xor == 0, 1.0, 0.0).astype(f32)
    X = [eye - jnp.where(xor == 1, L[b], 0.0) for b in blocks]
    for m in (2, 4, 8, 16, 32):
        level = (xor >= m) & (xor < 2 * m)
        Y = [mul3(X[b], jnp.where(level, L[b], 0.0)) for b in blocks]
        X = [X[b] - mul3(Y[b], X[b]) for b in blocks]
    UW, AUW, scal, Kt, sd = [], [], [], [], []
    for b in blocks:
        r = rs[b]
        rows, sc, kt, dd = [], [], [], []
        for h in range(4):
            c = h // 2
            cum = spreads[b][:, h * BLOCK:h * BLOCK + 1] + g[b * BLOCK:b * BLOCK + 1, 4 + h:5 + h]
            alive = start[r] < base + b * BLOCK
            s = jnp.where(alive, jnp.exp(cum), 0.0)
            last = cum[BLOCK - 1:]
            tail_start = start[(b + 1) * BLOCK - 1:(b + 1) * BLOCK]
            tr = jnp.where(pos[r] >= tail_start, jnp.exp(jnp.minimum(last - cum, 0.0)), 0.0)
            bt = beta[r, h:h + 1]
            rows.append(jnp.concatenate([bt * vs[h][r], bt * s * ks[c][r]], axis=1).astype(bf16))
            sc.append(s)
            kt.append(jnp.transpose(tr * ks[c][r]).astype(bf16))
            dd.append(s[BLOCK - 1:])
        UW.append(dotf(bdh(X[b]), jnp.concatenate(rows, axis=0)))
        scal.append(sc)
        Kt.append(kt)
        sd.append(dd)
    for b in blocks:
        AUW.append(dotf(bdh(A[b]), UW[b].astype(bf16)))
    state = [st_ref[h] for h in range(4)]
    for b in blocks:
        r = rs[b]
        for h in range(4):
            c = h // 2
            hr = slice(h * BLOCK, (h + 1) * BLOCK)
            P = scal[b][h] * qs[c][r] - AUW[b][hr, HD:]
            zp = jnp.concatenate([UW[b][hr, HD:].astype(bf16), P.astype(bf16)], axis=0)
            res = dotf(zp, state[h].astype(bf16))
            out_ref[r, h * HD:(h + 1) * HD] = AUW[b][hr, :HD] + res[BLOCK:, :HD]
            lift_ref[r, h * HD:(h + 1) * HD] = res[BLOCK:, HD:].astype(bf16)
            D = jnp.concatenate([UW[b][hr, :HD] - res[:BLOCK, :HD], -res[:BLOCK, HD:]], axis=1)
            dec = jnp.concatenate([sd[b][h], sd[b][h]], axis=1)
            state[h] = dec * state[h] + dotf(Kt[b][h], D.astype(bf16))
    for h in range(4):
        st_ref[h] = state[h]

def local_scan(info, q, k, v, halo, ba, dec, taps):
    n = q.shape[0]
    row = lambda w: pl.BlockSpec((ROWS, w), lambda i: (i, 0))
    whole = lambda s: pl.BlockSpec(s, lambda i: (0,) * len(s))
    return pl.pallas_call(
        local_kernel,
        grid=(n // ROWS,),
        in_specs=[pl.BlockSpec(memory_space=pltpu.SMEM), row(256), row(256), row(512),
                  whole((8, 1024)), row(8), whole((2, 8)), whole((4, 1024))],
        out_specs=[row(512), row(512), whole((4, HD, 2 * HD))],
        out_shape=[jax.ShapeDtypeStruct((n, 512), f32), jax.ShapeDtypeStruct((n, 512), bf16),
                   jax.ShapeDtypeStruct((4, HD, 2 * HD), f32)],
        scratch_shapes=[pltpu.VMEM((8, 1024), f32)],
        name="local_scan",
    )(info, q, k, v, halo, ba, dec, taps)
from jax.sharding import PartitionSpec as P

MESH = pl.DeviceIdType.MESH
TURNS = 8
SEQ = 16


def chain_kernel(t_ref, b_ref, in_ref, sent, held, send_sem, recv_sem):
    s = lax.axis_index("seq")
    after = lax.rem(s + 1, SEQ)
    barrier = pltpu.get_barrier_semaphore()
    pl.semaphore_signal(
        barrier, inc=1, device_id={"seq": lax.rem(s + SEQ - 1, SEQ)}, device_id_type=MESH)
    pl.semaphore_wait(barrier, 1)

    def hop(t, h):
        return pltpu.make_async_remote_copy(
            src_ref=sent.at[t, h], dst_ref=held.at[t, h], send_sem=send_sem.at[t, h],
            recv_sem=recv_sem.at[t, h], device_id={"seq": after}, device_id_type=MESH)

    for h in range(4):
        sent[0, h] = b_ref[h].astype(bf16)
        hop(0, h).start()

    def turn(t, carry):
        for h in range(4):
            hop(t - 1, h).wait_recv()
            arrived = held[t - 1, h]
            hi, lo = split2(t_ref[h])
            out = dotf(jnp.concatenate([hi, lo], axis=1),
                       jnp.concatenate([arrived, arrived], axis=0)) + b_ref[h]
            sent[t, h] = out.astype(bf16)
            hop(t, h).start()
        return carry

    lax.fori_loop(1, TURNS, turn, 0)
    for h in range(4):
        hop(TURNS - 1, h).wait_recv()
        in_ref[h] = held[TURNS - 1, h]

    def drain(t, carry):
        for h in range(4):
            hop(t, h).wait_send()
        return carry

    lax.fori_loop(0, TURNS, drain, 0)


def hand_over(across, local_state):
    vm = pl.BlockSpec(memory_space=pltpu.VMEM)
    return pl.pallas_call(
        chain_kernel,
        in_specs=[vm, vm], out_specs=vm,
        out_shape=jax.ShapeDtypeStruct((4, HD, HD), bf16),
        scratch_shapes=[pltpu.VMEM((TURNS, 4, HD, HD), bf16), pltpu.VMEM((TURNS, 4, HD, HD), bf16),
                        pltpu.SemaphoreType.DMA((TURNS, 4)), pltpu.SemaphoreType.DMA((TURNS, 4))],
        compiler_params=pltpu.CompilerParams(collective_id=1, has_side_effects=True),
        name="hand_over",
    )(across, local_state)


def gated_rows(o_ref, l_ref, s_ref, z_ref, nw_ref, r):
    cols = []
    for h in range(4):
        c = slice(h * HD, (h + 1) * HD)
        o = o_ref[r, c] + dotf(l_ref[r, c], s_ref[h])
        var = jnp.mean(o * o, axis=-1, keepdims=True)
        z = z_ref[r, c].astype(f32)
        cols.append((o * lax.rsqrt(var + 1e-06) * nw_ref[...] * (z * sigmoid(z))).astype(bf16))
    return jnp.concatenate(cols, axis=1)


def out_kernel(o_ref, l_ref, s_ref, z_ref, nw_ref, w_ref, p_ref):
    normed = gated_rows(o_ref, l_ref, s_ref, z_ref, nw_ref, slice(None))
    p_ref[...] = dotf(normed, w_ref[...]).astype(bf16)


def out_share(o, lift, s_in, z, nw, w):
    n = o.shape[0]
    row = lambda w: pl.BlockSpec((ROWS, w), lambda i: (i, 0))
    whole = lambda s: pl.BlockSpec(s, lambda i: (0,) * len(s))
    return pl.pallas_call(
        out_kernel, grid=(n // ROWS,),
        in_specs=[row(512), row(512), whole((4, HD, HD)), row(512), whole((1, HD)), whole((512, 2048))],
        out_specs=row(2048), out_shape=jax.ShapeDtypeStruct((n, 2048), bf16), name="out_share",
    )(o, lift, s_in, z, nw, w)


def per_device(hidden_in, w_query, w_key, w_value, w_gate, w_beta, w_alpha, dt_bias, head_decay,
               conv_query, conv_key, conv_value, norm_weight, w_out, prompt_lengths):
    n = hidden_in.shape[0]
    columns_in = lax.all_gather(hidden_in, "head", axis=1, tiled=True)
    q, k, v, z = (dotf(columns_in, w).astype(bf16) for w in (w_query, w_key, w_value, w_gate))
    ba = dotf(columns_in, jnp.concatenate([w_beta, w_alpha], axis=1))
    tails = jnp.concatenate([q[n - 8:], k[n - 8:], v[n - 8:]], axis=1)
    halo = lax.ppermute(tails, "seq", [(i, i + 1) for i in range(SEQ - 1)]).astype(f32)
    info = jnp.concatenate([jnp.reshape(lax.axis_index("seq") * n, (1,)), prompt_lengths]).astype(jnp.int32)
    zero4 = jnp.zeros((4,), f32)
    dec = jnp.stack([jnp.concatenate([zero4, dt_bias]), jnp.concatenate([zero4, -head_decay])])
    taps = jnp.concatenate([conv_query, conv_key, conv_value], axis=1).astype(f32)
    o, lift, st = local_scan(info, q, k, v, halo, ba, dec, taps)
    s_in = hand_over(st[:, :, HD:], st[:, :, :HD])
    part = out_share(o, lift, s_in, z, norm_weight[None, :], w_out)
    return lax.psum_scatter(part, "head", scatter_dimension=1, tiled=True)


def solution(mesh):
    rows, cols = P("seq", "head"), P(None, "head")
    in_specs = (rows, cols, cols, cols, cols, cols, cols, P("head"), P("head"), cols, cols, cols,
                P(), P("head", None), P())
    return jax.shard_map(per_device, mesh=mesh, in_specs=in_specs, out_specs=rows, check_vma=False)
```

```python
import functools
import jax
import jax.numpy as jnp
from jax import lax
from jax.experimental import pallas as pl
from jax.experimental.pallas import tpu as pltpu
BLOCK = 64
GROUP = 4
ROWS = BLOCK * GROUP
HD = 128
f32 = jnp.float32
bf16 = jnp.bfloat16

def dotf(a, b):
    return jnp.dot(a, b, preferred_element_type=f32)

def split2(x):
    hi = x.astype(bf16)
    return hi, (x - hi.astype(f32)).astype(bf16)

def sigmoid(x):
    return 1.0 / (1.0 + jnp.exp(-x))

def local_kernel(lens, dt, decay, q_ref, k_ref, v_ref, halo_ref, ba_ref, tq_ref, tk_ref, tv_ref,
                 out_ref, lift_ref, st_ref, carry):
    step = pl.program_id(0)

    @pl.when(step == 0)
    def _():
        rows = lax.broadcasted_iota(jnp.int32, (HD, 2 * HD), 0)
        cols = lax.broadcasted_iota(jnp.int32, (HD, 2 * HD), 1)
        init = jnp.where(cols - HD == rows, 1.0, 0.0).astype(f32)
        for h in range(4):
            st_ref[h] = init
        carry[...] = halo_ref[8:].astype(f32)

    base = (lax.axis_index("seq") * pl.num_programs(0) + step) * ROWS
    pos = base + lax.broadcasted_iota(jnp.int32, (ROWS, HD), 0)
    start = jnp.zeros((ROWS, HD), jnp.int32)
    off = lens[0] * 0
    for n in range(6):
        start = jnp.maximum(start, jnp.where(pos >= off, off, 0))
        off = off + lens[n]
    rel = pos - start
    keep = [None, rel >= 1, rel >= 2, rel >= 3]

    def conv(ref, tap_ref, c, w):
        x0 = ref[:, c * HD:(c + 1) * HD].astype(f32)
        x = jnp.concatenate([carry[:, w * HD:(w + 1) * HD], x0], axis=0)
        carry[:, w * HD:(w + 1) * HD] = x0[ROWS - 8:]
        taps = tap_ref[:, c * HD:(c + 1) * HD].astype(f32)
        y = taps[3:4] * x0
        for lag in (1, 2, 3):
            t = taps[3 - lag:4 - lag]
            y = y + jnp.where(keep[lag], t * x[8 - lag:8 - lag + ROWS], 0.0)
        return y * sigmoid(y)

    def unit(x):
        return x * lax.rsqrt(jnp.sum(x * x, axis=-1, keepdims=True) + 1e-06)

    qs = [unit(conv(q_ref, tq_ref, c, c)) * HD ** (-0.5) for c in range(2)]
    ks = [unit(conv(k_ref, tk_ref, c, 2 + c)) for c in range(2)]
    vs = [conv(v_ref, tv_ref, c, 4 + c) for c in range(4)]
    qb = [x.astype(bf16) for x in qs]
    kb = [x.astype(bf16) for x in ks]
    ba = ba_ref[...]
    beta = sigmoid(ba)
    lane = lax.broadcasted_iota(jnp.int32, (1, 8), 1)
    bias, rate = jnp.zeros((1, 8), f32), jnp.zeros((1, 8), f32)
    for h in range(4):
        bias = jnp.where(lane == 4 + h, dt[h], bias)
        rate = jnp.where(lane == 4 + h, -decay[h], rate)
    z = ba + bias
    g = rate * (jnp.maximum(z, 0.0) + jnp.log1p(jnp.exp(-jnp.abs(z))))

    ii = lax.broadcasted_iota(jnp.int32, (BLOCK, 256), 0)
    ll = lax.broadcasted_iota(jnp.int32, (BLOCK, 256), 1)
    jl = ll & (BLOCK - 1)
    xor = ii ^ jl
    head_of = ll >> 6
    low = lax.broadcasted_iota(jnp.int32, (BLOCK, HD), 1) < BLOCK
    ltri = jnp.where(
        lax.broadcasted_iota(jnp.int32, (BLOCK, BLOCK), 0)
        >= lax.broadcasted_iota(jnp.int32, (BLOCK, BLOCK), 1), 1.0, 0.0).astype(f32)
    hmask = [head_of == r for r in range(4)]

    def bd(m):
        z = jnp.zeros_like(m)
        return jnp.concatenate([jnp.where(hmask[r], m, z) for r in range(4)], axis=0)

    def packed(x, first, r):
        cols = [x[r, first + h:first + h + 1] for h in range(4)]
        return jnp.concatenate(
            [jnp.where(low, cols[0], cols[1]), jnp.where(low, cols[2], cols[3])], axis=1)

    def bdh(m):
        return bd(m).astype(bf16)

    def mul3(x, m):
        xh, xl = split2(x)
        mh = m.astype(bf16).astype(f32)
        ml = m - mh
        y = dotf(jnp.concatenate([xh, xl], axis=0), bdh(mh))
        return y[:BLOCK] + y[BLOCK:] + dotf(xh, bdh(ml))

    def mul1(x, m):
        return dotf(x.astype(bf16), bdh(m))

    blocks = range(GROUP)
    rs = [slice(b * BLOCK, (b + 1) * BLOCK) for b in blocks]
    L, A, spreads = [], [], []
    for b in blocks:
        r = rs[b]
        gm = jnp.where(ii > jl, packed(g, 4, r), 0.0)
        spread = jnp.dot(ltri, gm, precision=lax.Precision.HIGHEST, preferred_element_type=f32)
        spreads.append(spread)
        st2 = jnp.concatenate([start[r], start[r]], axis=1)
        mask = (ii >= jl) & (base + b * BLOCK + jl >= st2)
        factor = jnp.where(mask, jnp.exp(jnp.minimum(spread, 0.0)), 0.0)
        gr = []
        for c in range(2):
            kk = kb[c][r]
            gr.append(lax.dot_general(
                jnp.concatenate([kk, qb[c][r]], axis=0), jnp.concatenate([kk, kk], axis=0),
                (((1,), (1,)), ((), ())), preferred_element_type=f32))
        both = jnp.concatenate(gr, axis=1)
        L.append(jnp.where(ii > jl, packed(beta, 0, r) * factor * both[:BLOCK], 0.0))
        A.append(factor * both[BLOCK:])
    eye = jnp.where(xor == 0, 1.0, 0.0).astype(f32)
    X = [eye - jnp.where(xor == 1, L[b], 0.0) for b in blocks]
    for m in (2, 4, 8, 16, 32):
        level = (xor >= m) & (xor < 2 * m)
        Y = [mul3(X[b], jnp.where(level, L[b], 0.0)) for b in blocks]
        X = [X[b] - mul3(Y[b], X[b]) for b in blocks]
    UW, AUW, scal, Kt, sd = [], [], [], [], []
    for b in blocks:
        r = rs[b]
        rows, sc, kt, dd = [], [], [], []
        for h in range(4):
            c = h // 2
            cum = spreads[b][:, h * BLOCK:h * BLOCK + 1] + g[b * BLOCK:b * BLOCK + 1, 4 + h:5 + h]
            alive = start[r] < base + b * BLOCK
            s = jnp.where(alive, jnp.exp(cum), 0.0)
            last = cum[BLOCK - 1:]
            tail_start = start[(b + 1) * BLOCK - 1:(b + 1) * BLOCK]
            tr = jnp.where(pos[r] >= tail_start, jnp.exp(jnp.minimum(last - cum, 0.0)), 0.0)
            bt = beta[r, h:h + 1]
            rows.append(jnp.concatenate([bt * vs[h][r], bt * s * ks[c][r]], axis=1).astype(bf16))
            sc.append(s)
            kt.append(jnp.transpose(tr * ks[c][r]).astype(bf16))
            dd.append(s[BLOCK - 1:])
        UW.append(dotf(bdh(X[b]), jnp.concatenate(rows, axis=0)))
        scal.append(sc)
        Kt.append(kt)
        sd.append(dd)
    for b in blocks:
        AUW.append(dotf(bdh(A[b]), UW[b].astype(bf16)))
    state = [st_ref[h] for h in range(4)]
    for b in blocks:
        r = rs[b]
        for h in range(4):
            c = h // 2
            hr = slice(h * BLOCK, (h + 1) * BLOCK)
            P = scal[b][h] * qs[c][r] - AUW[b][hr, HD:]
            zp = jnp.concatenate([UW[b][hr, HD:].astype(bf16), P.astype(bf16)], axis=0)
            res = dotf(zp, state[h].astype(bf16))
            out_ref[r, h * HD:(h + 1) * HD] = AUW[b][hr, :HD] + res[BLOCK:, :HD]
            lift_ref[r, h * HD:(h + 1) * HD] = res[BLOCK:, HD:].astype(bf16)
            D = jnp.concatenate([UW[b][hr, :HD] - res[:BLOCK, :HD], -res[:BLOCK, HD:]], axis=1)
            dec = jnp.concatenate([sd[b][h], sd[b][h]], axis=1)
            state[h] = dec * state[h] + dotf(Kt[b][h], D.astype(bf16))
    for h in range(4):
        st_ref[h] = state[h]

def local_scan(lens, dt, decay, raw, halo, ba, tq, tk, tv):
    n = raw.shape[0]
    row = lambda w, j=0: pl.BlockSpec((ROWS, w), lambda i: (i, j))
    whole = lambda s: pl.BlockSpec(s, lambda i: (0,) * len(s))
    sm = pl.BlockSpec(memory_space=pltpu.SMEM)
    return pl.pallas_call(
        local_kernel,
        grid=(n // ROWS,),
        in_specs=[sm, sm, sm, row(256), row(256, 1), row(512, 1), whole((16, 1024)), row(8),
                  whole((4, 256)), whole((4, 256)), whole((4, 512))],
        out_specs=[row(512), row(512), whole((4, HD, 2 * HD))],
        out_shape=[jax.ShapeDtypeStruct((n, 512), f32), jax.ShapeDtypeStruct((n, 512), bf16),
                   jax.ShapeDtypeStruct((4, HD, 2 * HD), f32)],
        scratch_shapes=[pltpu.VMEM((8, 1024), f32)],
        name="local_scan",
    )(lens, dt, decay, raw, raw, raw, halo, ba, tq, tk, tv)
from jax.sharding import PartitionSpec as P

MESH = pl.DeviceIdType.MESH
TURNS = 8
SEQ = 16
CHIPS = 4
CHUNKS = 4
DEEP = 2048


class Later:
    def __init__(self, make):
        self.make = make

    def start(self):
        self.make().start()

    def wait(self):
        self.make().wait()

    def wait_recv(self):
        self.make().wait_recv()

    def wait_send(self):
        self.make().wait_send()


def ring_places():
    h = lax.axis_index("head")
    z, c = h // 2, lax.rem(h, 2)
    up = lax.rem(z + 1, CHIPS) * 2 + c
    down = lax.rem(z + CHIPS - 1, CHIPS) * 2 + c
    far = lax.rem(z + 2, CHIPS) * 2 + c
    return h, z, c, up, down, far, z * 2 + 1 - c


def greet(peers):
    barrier = pltpu.get_barrier_semaphore()
    for p in peers:
        pl.semaphore_signal(barrier, inc=1, device_id=p, device_id_type=MESH)
    pl.semaphore_wait(barrier, len(peers))


def project_kernel(x_ref, wq, wk, wv, wz, wb, wa, raw_hbm, ba_ref, halo_ref,
                   xg, w_all, wb_v, wa_v, raw_v, tail, landed, load_sem, store_sem, send_sem, recv_sem,
                   tail_sem):
    h, z, c, up, down, far, mate = ring_places()
    s = lax.axis_index("seq")
    n = x_ref.shape[0]
    rc = n // CHUNKS
    half = rc // 2
    loads = [pltpu.make_async_copy(a, b, load_sem.at[i]) for i, (a, b) in enumerate((
        (wq, w_all.at[:, 0:256]), (wk, w_all.at[:, 256:512]), (wv, w_all.at[:, 512:1024]),
        (wz, w_all.at[:, 1024:1536]), (wb, wb_v), (wa, wa_v)))]
    for cp in loads:
        cp.start()
    own = pl.ds(pl.multiple_of(h * 256, 256), 256)
    after = {"seq": lax.rem(s + 1, SEQ)}
    before = {"seq": lax.rem(s + SEQ - 1, SEQ)}
    greet([{"head": up}, {"head": down}, {"head": mate}, after, before])

    def cols(b):
        return pl.ds(pl.multiple_of(b * 256, 256), 256)

    def move(r, kind, src, rows, block, to):
        return Later(lambda: pltpu.make_async_remote_copy(
            src_ref=src, dst_ref=xg.at[rows, cols(block)], send_sem=send_sem.at[r, kind],
            recv_sem=recv_sem.at[r, kind], device_id={"head": to}, device_id_type=MESH))

    def rows_of(r):
        return pl.ds(r * rc, rc)

    def near(r):
        rows = rows_of(r)
        return [move(r, 0, x_ref.at[rows, :], rows, h, up), move(r, 1, x_ref.at[rows, :], rows, h, down),
                move(r, 2, x_ref.at[rows, :], rows, h, mate)]

    def relay(r):
        rows, ra, rb = rows_of(r), pl.ds(r * rc, half), pl.ds(r * rc + half, half)
        return [move(r, 3, xg.at[ra, cols(down)], ra, down, up),
                move(r, 4, xg.at[rb, cols(up)], rb, up, down),
                move(r, 5, xg.at[rows, cols(down)], rows, down, mate),
                move(r, 6, xg.at[rows, cols(up)], rows, up, mate)]

    def across(r):
        ra, rb = pl.ds(r * rc, half), pl.ds(r * rc + half, half)
        return [move(r, 7, xg.at[ra, cols(far)], ra, far, mate),
                move(r, 8, xg.at[rb, cols(far)], rb, far, mate)]

    order = [CHUNKS - 1] + list(range(CHUNKS - 1))
    for r in order:
        for cp in near(r):
            cp.start()
    xg[:, own] = x_ref[...]
    give = pltpu.make_async_remote_copy(
        src_ref=tail, dst_ref=landed, send_sem=tail_sem.at[0], recv_sem=tail_sem.at[1],
        device_id=after, device_id_type=MESH)

    def relay_stage(r):
        a, b, _ = near(r)
        fa, fb, ma, mb = relay(r)
        a.wait_recv()
        fa.start()
        ma.start()
        b.wait_recv()
        fb.start()
        mb.start()

    def across_stage(r):
        fa, fb, _, _ = relay(r)
        ca, cb = across(r)
        fa.wait_recv()
        ca.start()
        fb.wait_recv()
        cb.start()

    def multiply(i, r):
        near(r)[2].wait_recv()
        for cp in relay(r)[2:] + across(r):
            cp.wait_recv()
        if i == 0:
            for cp in loads:
                cp.wait()
        x = xg[r * rc:(r + 1) * rc, :]
        rs = slice(r * rc, (r + 1) * rc)
        ba_ref[rs, 0:4] = dotf(x, wb_v[...])
        ba_ref[rs, 4:8] = dotf(x, wa_v[...])
        for j in range(6):
            raw_v[rs, j * 256:(j + 1) * 256] = dotf(x, w_all[:, j * 256:(j + 1) * 256]).astype(bf16)
        if i == 0:
            tail[...] = raw_v[n - 16:, 0:1024]
            give.start()
        pltpu.make_async_copy(raw_v.at[rs, :], raw_hbm.at[rs, :], store_sem.at[r]).start()

    for i in range(CHUNKS + 2):
        if i < CHUNKS:
            relay_stage(order[i])
        if 1 <= i < CHUNKS + 1:
            across_stage(order[i - 1])
        if i >= 2:
            multiply(i - 2, order[i - 2])
    give.wait()
    halo_ref[...] = landed[...]
    for r in order:
        for cp in near(r) + relay(r) + across(r):
            cp.wait_send()
        rs = slice(r * rc, (r + 1) * rc)
        pltpu.make_async_copy(raw_v.at[rs, :], raw_hbm.at[rs, :], store_sem.at[r]).wait()


def project(x, wq, wk, wv, wz, wb, wa):
    n = x.shape[0]
    vm, anyw = pl.BlockSpec(memory_space=pltpu.VMEM), pl.BlockSpec(memory_space=pl.ANY)
    return pl.pallas_call(
        project_kernel,
        in_specs=[vm] + [anyw] * 6, out_specs=[anyw, vm, vm],
        out_shape=[jax.ShapeDtypeStruct((n, 1536), bf16), jax.ShapeDtypeStruct((n, 8), f32),
                   jax.ShapeDtypeStruct((16, 1024), bf16)],
        scratch_shapes=[
            pltpu.VMEM((n, DEEP), bf16), pltpu.VMEM((DEEP, 1536), bf16), pltpu.VMEM((DEEP, 4), bf16),
            pltpu.VMEM((DEEP, 4), bf16), pltpu.VMEM((n, 1536), bf16), pltpu.VMEM((16, 1024), bf16),
            pltpu.VMEM((16, 1024), bf16), pltpu.SemaphoreType.DMA((6,)), pltpu.SemaphoreType.DMA((CHUNKS,)),
            pltpu.SemaphoreType.DMA((CHUNKS, 9)), pltpu.SemaphoreType.DMA((CHUNKS, 9)),
            pltpu.SemaphoreType.DMA((2,))],
        compiler_params=pltpu.CompilerParams(collective_id=2, has_side_effects=True),
        name="project",
    )(x, wq, wk, wv, wz, wb, wa)


def chain(t_of, b_of, sent, held, send_sem, recv_sem, after):
    def hop(t, h):
        return pltpu.make_async_remote_copy(
            src_ref=sent.at[t, h], dst_ref=held.at[t, h], send_sem=send_sem.at[t, h],
            recv_sem=recv_sem.at[t, h], device_id=after, device_id_type=MESH)

    for h in range(4):
        sent[0, h] = b_of(h).astype(bf16)
        hop(0, h).start()

    def turn(t, carry):
        for h in range(4):
            hop(t - 1, h).wait_recv()
            arrived = held[t - 1, h]
            hi, lo = split2(t_of(h))
            out = dotf(jnp.concatenate([hi, lo], axis=1),
                       jnp.concatenate([arrived, arrived], axis=0)) + b_of(h)
            sent[t, h] = out.astype(bf16)
            hop(t, h).start()
        return carry

    lax.fori_loop(1, TURNS, turn, 0)
    for h in range(4):
        hop(TURNS - 1, h).wait_recv()

    def drain(t, carry):
        for h in range(4):
            hop(t, h).wait_send()
        return carry

    return [held[TURNS - 1, h] for h in range(4)], lambda: lax.fori_loop(0, TURNS, drain, 0)


def output_kernel(st_ref, o_hbm, l_hbm, raw_hbm, nw_ref, w_hbm, out_ref,
                  o_v, l_v, z_v, w_v, sent, held, mine, theirs, given, pass_out, pass_in, to_up, to_down,
                  from_down, from_up, load_sem, c_send, c_recv, p_send, p_recv, send_sem, recv_sem):
    h, z, c, up, down, far, mate = ring_places()
    s = lax.axis_index("seq")
    n = o_v.shape[0]
    rc = n // CHUNKS
    half = rc // 2
    loads = [pltpu.make_async_copy(a, b, load_sem.at[i]) for i, (a, b) in enumerate((
        (o_hbm, o_v), (l_hbm, l_v), (raw_hbm.at[:, 1024:1536], z_v), (w_hbm, w_v)))]
    for cp in loads:
        cp.start()
    after = {"seq": lax.rem(s + 1, SEQ)}
    before = {"seq": lax.rem(s + SEQ - 1, SEQ)}
    greet([{"head": up}, {"head": down}, {"head": mate}, after, before])
    s_in, drained = chain(lambda i: st_ref[i, :, HD:], lambda i: st_ref[i, :, :HD],
                          sent, held, c_send, c_recv, after)
    for cp in loads:
        cp.wait()

    def remote(src, dst, ss, rs, to):
        return Later(lambda: pltpu.make_async_remote_copy(
            src_ref=src, dst_ref=dst, send_sem=ss, recv_sem=rs, device_id={"head": to},
            device_id_type=MESH))

    def swap(r, j):
        return remote(given.at[r, j], theirs.at[r, j], p_send.at[r, j], p_recv.at[r, j], mate)

    def copies(r):
        a, b = pl.ds(0, half), pl.ds(half, half)
        sem = lambda k: (send_sem.at[r, k], recv_sem.at[r, k])
        return [remote(pass_out.at[r, a], pass_in.at[r, a], *sem(0), up),
                remote(pass_out.at[r, b], pass_in.at[r, b], *sem(1), down),
                remote(to_up.at[r, b], from_down.at[r, b], *sem(2), up),
                remote(to_down.at[r, a], from_up.at[r, a], *sem(3), down),
                remote(to_up.at[r, a], from_down.at[r, a], *sem(4), up),
                remote(to_down.at[r, b], from_up.at[r, b], *sem(5), down)]

    def wcols(b):
        return pl.ds(pl.multiple_of(b * 256, 256), 256)

    def chip(j):
        return lax.rem(z + j, CHIPS)

    def share(r):
        rs = slice(r * rc, (r + 1) * rc)
        parts = []
        for i in range(4):
            hc = slice(i * HD, (i + 1) * HD)
            o = o_v[rs, hc] + dotf(l_v[rs, hc], s_in[i])
            var = jnp.mean(o * o, axis=-1, keepdims=True)
            g = z_v[rs, hc].astype(f32)
            parts.append((o * lax.rsqrt(var + 1e-06) * nw_ref[...] * (g * sigmoid(g))).astype(bf16))
        normed = jnp.concatenate(parts, axis=1)
        for j in (2, 1, 3, 0):
            given[r, j] = dotf(normed, w_v[:, wcols(chip(j) * 2 + 1 - c)]).astype(bf16)
            swap(r, j).start()
        for j in (2, 1, 3, 0):
            mine[r, j] = dotf(normed, w_v[:, wcols(chip(j) * 2 + c)])

    def both(r, j):
        return mine[r, j] + theirs[r, j].astype(f32)

    def leave(r):
        cps = copies(r)
        swap(r, 2).wait_recv()
        pass_out[r] = both(r, 2).astype(bf16)
        cps[0].start()
        cps[1].start()
        swap(r, 1).wait_recv()
        to_up[r, half:] = both(r, 1)[half:].astype(bf16)
        cps[2].start()
        swap(r, 3).wait_recv()
        to_down[r, :half] = both(r, 3)[:half].astype(bf16)
        cps[3].start()

    def add_on(r):
        cps = copies(r)
        cps[0].wait_recv()
        to_up[r, :half] = (both(r, 1)[:half] + pass_in[r, :half].astype(f32)).astype(bf16)
        cps[4].start()
        cps[1].wait_recv()
        to_down[r, half:] = (both(r, 3)[half:] + pass_in[r, half:].astype(f32)).astype(bf16)
        cps[5].start()

    def finish(r):
        for cp in copies(r)[2:]:
            cp.wait_recv()
        swap(r, 0).wait_recv()
        out_ref[r * rc:(r + 1) * rc, :] = (
            both(r, 0) + from_down[r].astype(f32) + from_up[r].astype(f32)).astype(bf16)

    for i in range(CHUNKS + 3):
        if i < CHUNKS:
            share(i)
        if 1 <= i < CHUNKS + 1:
            leave(i - 1)
        if 2 <= i < CHUNKS + 2:
            add_on(i - 2)
        if i >= 3:
            finish(i - 3)
    drained()
    for r in range(CHUNKS):
        for j in range(4):
            swap(r, j).wait_send()
        for cp in copies(r):
            cp.wait_send()


def output(st, o, lift, raw, nw, w):
    n = o.shape[0]
    rc = n // CHUNKS
    vm, anyw = pl.BlockSpec(memory_space=pltpu.VMEM), pl.BlockSpec(memory_space=pl.ANY)
    buf = pltpu.VMEM((CHUNKS, rc, 256), bf16)
    dma = pltpu.SemaphoreType.DMA
    return pl.pallas_call(
        output_kernel,
        in_specs=[vm, anyw, anyw, anyw, vm, anyw], out_specs=vm,
        out_shape=jax.ShapeDtypeStruct((n, 256), bf16),
        scratch_shapes=[
            pltpu.VMEM((n, 512), f32), pltpu.VMEM((n, 512), bf16), pltpu.VMEM((n, 512), bf16),
            pltpu.VMEM((512, 2048), bf16), pltpu.VMEM((TURNS, 4, HD, HD), bf16),
            pltpu.VMEM((TURNS, 4, HD, HD), bf16), pltpu.VMEM((CHUNKS, 4, rc, 256), f32),
            pltpu.VMEM((CHUNKS, 4, rc, 256), bf16), pltpu.VMEM((CHUNKS, 4, rc, 256), bf16),
            buf, buf, buf, buf, buf, buf,
            dma((4,)), dma((TURNS, 4)), dma((TURNS, 4)), dma((CHUNKS, 4)), dma((CHUNKS, 4)),
            dma((CHUNKS, 6)), dma((CHUNKS, 6))],
        compiler_params=pltpu.CompilerParams(collective_id=3, has_side_effects=True),
        name="output",
    )(st, o, lift, raw, nw, w)


def per_device(hidden_in, w_query, w_key, w_value, w_gate, w_beta, w_alpha, dt_bias, head_decay,
               conv_query, conv_key, conv_value, norm_weight, w_out, prompt_lengths):
    raw, ba, halo = project(hidden_in, w_query, w_key, w_value, w_gate, w_beta, w_alpha)
    o, lift, st = local_scan(prompt_lengths, dt_bias, head_decay, raw, halo, ba,
                             conv_query, conv_key, conv_value)
    return output(st, o, lift, raw, norm_weight[None, :], w_out)


def solution(mesh):
    rows, cols = P("seq", "head"), P(None, "head")
    in_specs = (rows, cols, cols, cols, cols, cols, cols, P("head"), P("head"), cols, cols, cols,
                P(), P("head", None), P())
    return jax.shard_map(per_device, mesh=mesh, in_specs=in_specs, out_specs=rows, check_vma=False)
```

```python
import functools
import jax
import jax.numpy as jnp
from jax import lax
from jax.experimental import pallas as pl
from jax.experimental.pallas import tpu as pltpu
BLOCK = 64
GROUP = 4
ROWS = BLOCK * GROUP
HD = 128
f32 = jnp.float32
bf16 = jnp.bfloat16

def dotf(a, b):
    return jnp.dot(a, b, preferred_element_type=f32)

def split2(x):
    hi = x.astype(bf16)
    return hi, (x - hi.astype(f32)).astype(bf16)

def sigmoid(x):
    return 1.0 / (1.0 + jnp.exp(-x))

def scan_rows(base, lens, dt, decay, q_ref, k_ref, v_ref, ba_ref, tq_ref, tk_ref, tv_ref,
              out_ref, lift_ref, st_ref, carry):
    pos = base + lax.broadcasted_iota(jnp.int32, (ROWS, HD), 0)
    start = jnp.zeros((ROWS, HD), jnp.int32)
    off = lens[0] * 0
    for n in range(6):
        start = jnp.maximum(start, jnp.where(pos >= off, off, 0))
        off = off + lens[n]
    rel = pos - start
    keep = [None, rel >= 1, rel >= 2, rel >= 3]

    def conv(ref, tap_ref, c, w):
        x0 = ref[:, c * HD:(c + 1) * HD].astype(f32)
        x = jnp.concatenate([carry[:, w * HD:(w + 1) * HD], x0], axis=0)
        carry[:, w * HD:(w + 1) * HD] = x0[ROWS - 8:]
        taps = tap_ref[:, c * HD:(c + 1) * HD].astype(f32)
        y = taps[3:4] * x0
        for lag in (1, 2, 3):
            t = taps[3 - lag:4 - lag]
            y = y + jnp.where(keep[lag], t * x[8 - lag:8 - lag + ROWS], 0.0)
        return y * sigmoid(y)

    def unit(x):
        return x * lax.rsqrt(jnp.sum(x * x, axis=-1, keepdims=True) + 1e-06)

    qs = [unit(conv(q_ref, tq_ref, c, c)) * HD ** (-0.5) for c in range(2)]
    ks = [unit(conv(k_ref, tk_ref, c, 2 + c)) for c in range(2)]
    vs = [conv(v_ref, tv_ref, c, 4 + c) for c in range(4)]
    qb = [x.astype(bf16) for x in qs]
    kb = [x.astype(bf16) for x in ks]
    ba = ba_ref[...]
    beta = sigmoid(ba)
    lane = lax.broadcasted_iota(jnp.int32, (1, 8), 1)
    bias, rate = jnp.zeros((1, 8), f32), jnp.zeros((1, 8), f32)
    for h in range(4):
        bias = jnp.where(lane == 4 + h, dt[h], bias)
        rate = jnp.where(lane == 4 + h, -decay[h], rate)
    z = ba + bias
    g = rate * (jnp.maximum(z, 0.0) + jnp.log1p(jnp.exp(-jnp.abs(z))))

    ii = lax.broadcasted_iota(jnp.int32, (BLOCK, 256), 0)
    ll = lax.broadcasted_iota(jnp.int32, (BLOCK, 256), 1)
    jl = ll & (BLOCK - 1)
    xor = ii ^ jl
    head_of = ll >> 6
    low = lax.broadcasted_iota(jnp.int32, (BLOCK, HD), 1) < BLOCK
    ltri = jnp.where(
        lax.broadcasted_iota(jnp.int32, (BLOCK, BLOCK), 0)
        >= lax.broadcasted_iota(jnp.int32, (BLOCK, BLOCK), 1), 1.0, 0.0).astype(f32)
    hmask = [head_of == r for r in range(4)]

    def bd(m):
        z = jnp.zeros_like(m)
        return jnp.concatenate([jnp.where(hmask[r], m, z) for r in range(4)], axis=0)

    def packed(x, first, r):
        cols = [x[r, first + h:first + h + 1] for h in range(4)]
        return jnp.concatenate(
            [jnp.where(low, cols[0], cols[1]), jnp.where(low, cols[2], cols[3])], axis=1)

    def bdh(m):
        return bd(m).astype(bf16)

    def mul3(x, m):
        xh, xl = split2(x)
        mh = m.astype(bf16).astype(f32)
        ml = m - mh
        y = dotf(jnp.concatenate([xh, xl], axis=0), bdh(mh))
        return y[:BLOCK] + y[BLOCK:] + dotf(xh, bdh(ml))

    def mul1(x, m):
        return dotf(x.astype(bf16), bdh(m))

    blocks = range(GROUP)
    rs = [slice(b * BLOCK, (b + 1) * BLOCK) for b in blocks]
    L, A, spreads = [], [], []
    for b in blocks:
        r = rs[b]
        gm = jnp.where(ii > jl, packed(g, 4, r), 0.0)
        spread = jnp.dot(ltri, gm, precision=lax.Precision.HIGHEST, preferred_element_type=f32)
        spreads.append(spread)
        st2 = jnp.concatenate([start[r], start[r]], axis=1)
        mask = (ii >= jl) & (base + b * BLOCK + jl >= st2)
        factor = jnp.where(mask, jnp.exp(jnp.minimum(spread, 0.0)), 0.0)
        gr = []
        for c in range(2):
            kk = kb[c][r]
            gr.append(lax.dot_general(
                jnp.concatenate([kk, qb[c][r]], axis=0), jnp.concatenate([kk, kk], axis=0),
                (((1,), (1,)), ((), ())), preferred_element_type=f32))
        both = jnp.concatenate(gr, axis=1)
        L.append(jnp.where(ii > jl, packed(beta, 0, r) * factor * both[:BLOCK], 0.0))
        A.append(factor * both[BLOCK:])
    eye = jnp.where(xor == 0, 1.0, 0.0).astype(f32)
    X = [eye - jnp.where(xor == 1, L[b], 0.0) for b in blocks]
    for m in (2, 4, 8, 16, 32):
        level = (xor >= m) & (xor < 2 * m)
        Y = [mul3(X[b], jnp.where(level, L[b], 0.0)) for b in blocks]
        X = [X[b] - mul3(Y[b], X[b]) for b in blocks]
    UW, AUW, scal, Kt, sd = [], [], [], [], []
    for b in blocks:
        r = rs[b]
        rows, sc, kt, dd = [], [], [], []
        for h in range(4):
            c = h // 2
            cum = spreads[b][:, h * BLOCK:h * BLOCK + 1] + g[b * BLOCK:b * BLOCK + 1, 4 + h:5 + h]
            alive = start[r] < base + b * BLOCK
            s = jnp.where(alive, jnp.exp(cum), 0.0)
            last = cum[BLOCK - 1:]
            tail_start = start[(b + 1) * BLOCK - 1:(b + 1) * BLOCK]
            tr = jnp.where(pos[r] >= tail_start, jnp.exp(jnp.minimum(last - cum, 0.0)), 0.0)
            bt = beta[r, h:h + 1]
            rows.append(jnp.concatenate([bt * vs[h][r], bt * s * ks[c][r]], axis=1).astype(bf16))
            sc.append(s)
            kt.append(jnp.transpose(tr * ks[c][r]).astype(bf16))
            dd.append(s[BLOCK - 1:])
        UW.append(dotf(bdh(X[b]), jnp.concatenate(rows, axis=0)))
        scal.append(sc)
        Kt.append(kt)
        sd.append(dd)
    for b in blocks:
        AUW.append(dotf(bdh(A[b]), UW[b].astype(bf16)))
    state = [st_ref[h] for h in range(4)]
    for b in blocks:
        r = rs[b]
        for h in range(4):
            c = h // 2
            hr = slice(h * BLOCK, (h + 1) * BLOCK)
            P = scal[b][h] * qs[c][r] - AUW[b][hr, HD:]
            zp = jnp.concatenate([UW[b][hr, HD:].astype(bf16), P.astype(bf16)], axis=0)
            res = dotf(zp, state[h].astype(bf16))
            out_ref[r, h * HD:(h + 1) * HD] = AUW[b][hr, :HD] + res[BLOCK:, :HD]
            lift_ref[r, h * HD:(h + 1) * HD] = res[BLOCK:, HD:].astype(bf16)
            D = jnp.concatenate([UW[b][hr, :HD] - res[:BLOCK, :HD], -res[:BLOCK, HD:]], axis=1)
            dec = jnp.concatenate([sd[b][h], sd[b][h]], axis=1)
            state[h] = dec * state[h] + dotf(Kt[b][h], D.astype(bf16))
    for h in range(4):
        st_ref[h] = state[h]


from jax.sharding import PartitionSpec as P

MESH = pl.DeviceIdType.MESH
SIDE = 4
OUT_CHUNKS = 8
SEQ = 16
CHIPS = 4
CHUNKS = 4
DEEP = 2048


class Later:
    def __init__(self, make):
        self.make = make

    def start(self):
        self.make().start()

    def wait(self):
        self.make().wait()

    def wait_recv(self):
        self.make().wait_recv()

    def wait_send(self):
        self.make().wait_send()


def ring_places():
    h = lax.axis_index("head")
    z, c = h // 2, lax.rem(h, 2)
    up = lax.rem(z + 1, CHIPS) * 2 + c
    down = lax.rem(z + CHIPS - 1, CHIPS) * 2 + c
    far = lax.rem(z + 2, CHIPS) * 2 + c
    return h, z, c, up, down, far, z * 2 + 1 - c


def greet(peers):
    barrier = pltpu.get_barrier_semaphore()
    for p in peers:
        pl.semaphore_signal(barrier, inc=1, device_id=p, device_id_type=MESH)
    pl.semaphore_wait(barrier, len(peers))


def project_kernel(lens, dt, decay, x_ref, wq, wk, wv, wz, wb, wa, tq_ref, tk_ref, tv_ref,
                   o_hbm, l_hbm, z_hbm, st_ref,
                   xg, w_all, wb_v, wa_v, wba, raw_v, ba_v, o_v, l_v, carry, tail, landed,
                   load_sem, store_sem, send_sem, recv_sem, tail_sem):
    h, z, c, up, down, far, mate = ring_places()
    s = lax.axis_index("seq")
    n = x_ref.shape[0]
    rc = n // CHUNKS
    half = rc // 2
    loads = [pltpu.make_async_copy(a, b, load_sem.at[i]) for i, (a, b) in enumerate((
        (wq, w_all.at[:, 0:256]), (wk, w_all.at[:, 256:512]), (wv, w_all.at[:, 512:1024]),
        (wz, w_all.at[:, 1024:1536]), (wb, wb_v), (wa, wa_v)))]
    for cp in loads:
        cp.start()
    own = pl.ds(pl.multiple_of(h * 256, 256), 256)
    after = {"seq": lax.rem(s + 1, SEQ)}
    before = {"seq": lax.rem(s + SEQ - 1, SEQ)}
    greet([{"head": up}, {"head": down}, {"head": mate}, after, before])

    def cols(b):
        return pl.ds(pl.multiple_of(b * 256, 256), 256)

    def move(r, kind, src, rows, block, to):
        return Later(lambda: pltpu.make_async_remote_copy(
            src_ref=src, dst_ref=xg.at[rows, cols(block)], send_sem=send_sem.at[r, kind],
            recv_sem=recv_sem.at[r, kind], device_id={"head": to}, device_id_type=MESH))

    def span(first, size):
        return pl.ds(pl.multiple_of(first, size), size)

    def rows_of(r):
        return span(r * rc, rc)

    def near(r):
        rows = rows_of(r)
        return [move(r, 0, x_ref.at[rows, :], rows, h, up), move(r, 1, x_ref.at[rows, :], rows, h, down),
                move(r, 2, x_ref.at[rows, :], rows, h, mate)]

    def relay(r):
        rows, ra, rb = rows_of(r), span(r * rc, half), span(r * rc + half, half)
        return [move(r, 3, xg.at[ra, cols(down)], ra, down, up),
                move(r, 4, xg.at[rb, cols(up)], rb, up, down),
                move(r, 5, xg.at[rows, cols(down)], rows, down, mate),
                move(r, 6, xg.at[rows, cols(up)], rows, up, mate)]

    def across(r):
        ra, rb = span(r * rc, half), span(r * rc + half, half)
        return [move(r, 7, xg.at[ra, cols(far)], ra, far, mate),
                move(r, 8, xg.at[rb, cols(far)], rb, far, mate)]

    def place(i):
        return lax.rem(i + CHUNKS - 1, CHUNKS)

    for i in (0, 1):
        for cp in near(place(i)):
            cp.start()
    xg[:, own] = x_ref[...]
    rows_i = lax.broadcasted_iota(jnp.int32, (HD, 2 * HD), 0)
    cols_i = lax.broadcasted_iota(jnp.int32, (HD, 2 * HD), 1)
    for i in range(4):
        st_ref[i] = jnp.where(cols_i - HD == rows_i, 1.0, 0.0).astype(f32)
    give = Later(lambda: pltpu.make_async_remote_copy(
        src_ref=tail, dst_ref=landed, send_sem=tail_sem.at[0], recv_sem=tail_sem.at[1],
        device_id=after, device_id_type=MESH))

    def relay_stage(r):
        a, b, _ = near(r)
        fa, fb, ma, mb = relay(r)
        a.wait_recv()
        fa.start()
        ma.start()
        b.wait_recv()
        fb.start()
        mb.start()

    def across_stage(r):
        fa, fb, _, _ = relay(r)
        ca, cb = across(r)
        fa.wait_recv()
        ca.start()
        fb.wait_recv()
        cb.start()

    def stores(r):
        rows = rows_of(r)
        return [Later(lambda a=a, b=b, j=j: pltpu.make_async_copy(a, b, store_sem.at[r, j]))
                for j, (a, b) in enumerate((
                    (o_v.at[rows, :], o_hbm.at[rows, :]), (l_v.at[rows, :], l_hbm.at[rows, :]),
                    (raw_v.at[rows, 1024:1536], z_hbm.at[rows, :])))]

    def multiply(r):
        near(r)[2].wait_recv()
        for cp in relay(r)[2:] + across(r):
            cp.wait_recv()
        rs = rows_of(r)
        x = xg[rs, :]
        ba_v[rs, :] = lax.dot_general(x, wba[...], (((1,), (1,)), ((), ())), preferred_element_type=f32)
        for j in range(6):
            raw_v[rs, j * 256:(j + 1) * 256] = dotf(x, w_all[:, j * 256:(j + 1) * 256]).astype(bf16)

    def scan(r):
        rs = rows_of(r)
        scan_rows((s * CHUNKS + r) * rc, lens, dt, decay, raw_v.at[rs, 0:256], raw_v.at[rs, 256:512],
                  raw_v.at[rs, 512:1024], ba_v.at[rs, :], tq_ref, tk_ref, tv_ref,
                  o_v.at[rs, :], l_v.at[rs, :], st_ref, carry)
        for cp in stores(r):
            cp.start()

    def stage(i, none):
        @pl.when(i < CHUNKS)
        def _():
            relay_stage(place(i))

        @pl.when(i + 2 < CHUNKS)
        def _():
            for cp in near(place(i + 2)):
                cp.start()

        @pl.when((i >= 1) & (i < CHUNKS + 1))
        def _():
            across_stage(place(i + CHUNKS - 1))

        @pl.when(i == 2)
        def _():
            for cp in loads:
                cp.wait()
            wba[...] = jnp.concatenate(
                [wb_v[...].astype(f32), wa_v[...].astype(f32)], axis=0).astype(bf16)

        @pl.when((i >= 2) & (i < CHUNKS + 2))
        def _():
            multiply(place(i + CHUNKS - 2))

        @pl.when(i == 2)
        def _():
            tail[...] = raw_v[n - 16:, 0:1024]
            give.start()

        @pl.when(i == 3)
        def _():
            give.wait_recv()
            carry[...] = landed[8:].astype(f32)

        @pl.when(i >= 3)
        def _():
            scan(i - 3)
        return none

    lax.fori_loop(0, CHUNKS + 3, stage, 0)
    give.wait_send()

    def drain(r, none):
        for cp in near(r) + relay(r) + across(r):
            cp.wait_send()
        for cp in stores(r):
            cp.wait()
        return none

    lax.fori_loop(0, CHUNKS, drain, 0)


def project(lens, dt, decay, x, wq, wk, wv, wz, wb, wa, tq, tk, tv):
    n = x.shape[0]
    vm, anyw = pl.BlockSpec(memory_space=pltpu.VMEM), pl.BlockSpec(memory_space=pl.ANY)
    sm = pl.BlockSpec(memory_space=pltpu.SMEM)
    dma = pltpu.SemaphoreType.DMA
    return pl.pallas_call(
        project_kernel,
        in_specs=[sm, sm, sm, vm] + [anyw] * 6 + [vm] * 3, out_specs=[anyw, anyw, anyw, vm],
        out_shape=[jax.ShapeDtypeStruct((n, 512), f32), jax.ShapeDtypeStruct((n, 512), bf16),
                   jax.ShapeDtypeStruct((n, 512), bf16), jax.ShapeDtypeStruct((4, HD, 2 * HD), f32)],
        scratch_shapes=[
            pltpu.VMEM((n, DEEP), bf16), pltpu.VMEM((DEEP, 1536), bf16), pltpu.VMEM((4, DEEP), bf16),
            pltpu.VMEM((4, DEEP), bf16), pltpu.VMEM((8, DEEP), bf16), pltpu.VMEM((n, 1536), bf16),
            pltpu.VMEM((n, 8), f32), pltpu.VMEM((n, 512), f32), pltpu.VMEM((n, 512), bf16),
            pltpu.VMEM((8, 1024), f32), pltpu.VMEM((16, 1024), bf16), pltpu.VMEM((16, 1024), bf16),
            dma((6,)), dma((CHUNKS, 3)), dma((CHUNKS, 9)), dma((CHUNKS, 9)), dma((2,))],
        compiler_params=pltpu.CompilerParams(collective_id=2, has_side_effects=True),
        name="project",
    )(lens, dt, decay, x, wq, wk, wv, wz, wb, wa, tq, tk, tv)


def hand_over(st_ref, s, g_out, g_in, t_out, t_in, b_in, r_out, r_in, h_send, h_recv):
    x, y = s // SIDE, lax.rem(s, SIDE)
    row = lambda j: x * SIDE + lax.rem(y + j, SIDE)
    col = lambda j: lax.rem(x + j, SIDE) * SIDE + y

    def to(k, src, dst, place):
        return Later(lambda: pltpu.make_async_remote_copy(
            src_ref=src, dst_ref=dst, send_sem=h_send.at[k], recv_sem=h_recv.at[k],
            device_id={"seq": place}, device_id_type=MESH))

    gather = [to(j - 1, g_out.at[lax.rem(y + j, SIDE)], g_in.at[j], row(j)) for j in (1, 2, 3)]
    totals = [to(3, t_out, t_in, col(1)), to(4, t_out.at[:, :HD], b_in, col(2))]
    back = [to(4 + j, r_out.at[lax.rem(y + j, SIDE)], r_in.at[j], row(j)) for j in (1, 2, 3)]
    for h in range(4):
        g_out[h] = st_ref[h].astype(bf16)
    for j in (1, 0, 2):
        gather[j].start()
    g_in[0] = g_out[y]
    for cp in gather:
        cp.wait_recv()
    prefix = [None, g_in[lax.rem(y + SIDE, SIDE)].astype(f32)]
    for i in (1, 2, 3):
        g = g_in[lax.rem(y + SIDE - i, SIDE)]
        nxt = dotf(g[:, HD:], prefix[i].astype(bf16))
        prefix.append(nxt + jnp.concatenate(
            [g[:, :HD].astype(f32), jnp.zeros((HD, HD), f32)], axis=1))
    t_out[...] = prefix[4].astype(bf16)
    totals[1].start()
    totals[0].start()
    for cp in totals:
        cp.wait_recv()
    before = dotf(t_in[:, HD:], b_in[...]) + t_in[:, :HD].astype(f32)
    before = before.astype(bf16)
    r_out[0] = before
    for i in (1, 2, 3):
        r_out[i] = (prefix[i][:, :HD] + dotf(prefix[i][:, HD:].astype(bf16), before)).astype(bf16)
    for j in (1, 0, 2):
        back[j].start()
    r_in[0] = r_out[y]
    for cp in back:
        cp.wait_recv()

    def drain():
        for cp in gather + totals + back:
            cp.wait_send()

    return [r_in[lax.rem(y + SIDE - h, SIDE)] for h in range(4)], drain


def output_kernel(st_ref, o_hbm, l_hbm, z_hbm, nw_ref, w_hbm, out_ref,
                  o_v, l_v, z_v, w_v, g_out, g_in, t_out, t_in, b_in, r_out, r_in, mine, theirs, given, pass_out, pass_in, to_up, to_down,
                  from_down, from_up, load_sem, h_send, h_recv, p_send, p_recv, send_sem, recv_sem):
    h, z, c, up, down, far, mate = ring_places()
    s = lax.axis_index("seq")
    n = o_v.shape[0]
    rc = n // OUT_CHUNKS
    half = rc // 2
    loads = [pltpu.make_async_copy(a, b, load_sem.at[i]) for i, (a, b) in enumerate((
        (o_hbm, o_v), (l_hbm, l_v), (z_hbm, z_v), (w_hbm, w_v)))]
    for cp in loads:
        cp.start()
    x, y = s // SIDE, lax.rem(s, SIDE)
    greet([{"head": up}, {"head": down}, {"head": mate}]
          + [{"seq": x * SIDE + lax.rem(y + j, SIDE)} for j in (1, 2, 3)]
          + [{"seq": lax.rem(x + j, SIDE) * SIDE + y} for j in (1, 2, 3)])
    s_in, drained = hand_over(st_ref, s, g_out, g_in, t_out, t_in, b_in, r_out, r_in, h_send, h_recv)
    for cp in loads:
        cp.wait()

    def remote(src, dst, ss, rs, to):
        return Later(lambda: pltpu.make_async_remote_copy(
            src_ref=src, dst_ref=dst, send_sem=ss, recv_sem=rs, device_id={"head": to},
            device_id_type=MESH))

    def swap(r, j):
        return remote(given.at[r, j], theirs.at[r, j], p_send.at[r, j], p_recv.at[r, j], mate)

    def copies(r):
        a, b = pl.ds(0, half), pl.ds(half, half)
        sem = lambda k: (send_sem.at[r, k], recv_sem.at[r, k])
        return [remote(pass_out.at[r, a], pass_in.at[r, a], *sem(0), up),
                remote(pass_out.at[r, b], pass_in.at[r, b], *sem(1), down),
                remote(to_up.at[r, b], from_down.at[r, b], *sem(2), up),
                remote(to_down.at[r, a], from_up.at[r, a], *sem(3), down),
                remote(to_up.at[r, a], from_down.at[r, a], *sem(4), up),
                remote(to_down.at[r, b], from_up.at[r, b], *sem(5), down)]

    def wcols(b):
        return pl.ds(pl.multiple_of(b * 256, 256), 256)

    def chip(j):
        return lax.rem(z + j, CHIPS)

    def share(r):
        rs = slice(r * rc, (r + 1) * rc)
        parts = []
        for i in range(4):
            hc = slice(i * HD, (i + 1) * HD)
            o = o_v[rs, hc] + dotf(l_v[rs, hc], s_in[i])
            var = jnp.mean(o * o, axis=-1, keepdims=True)
            g = z_v[rs, hc].astype(f32)
            parts.append((o * lax.rsqrt(var + 1e-06) * nw_ref[...] * (g * sigmoid(g))).astype(bf16))
        normed = jnp.concatenate(parts, axis=1)
        for j in (2, 1, 3, 0):
            given[r, j] = dotf(normed, w_v[:, wcols(chip(j) * 2 + 1 - c)]).astype(bf16)
            swap(r, j).start()
        for j in (2, 1, 3, 0):
            mine[r, j] = dotf(normed, w_v[:, wcols(chip(j) * 2 + c)])

    def both(r, j):
        return mine[r, j] + theirs[r, j].astype(f32)

    def leave(r):
        cps = copies(r)
        swap(r, 2).wait_recv()
        pass_out[r] = both(r, 2).astype(bf16)
        cps[0].start()
        cps[1].start()
        swap(r, 1).wait_recv()
        to_up[r, half:] = both(r, 1)[half:].astype(bf16)
        cps[2].start()
        swap(r, 3).wait_recv()
        to_down[r, :half] = both(r, 3)[:half].astype(bf16)
        cps[3].start()

    def add_on(r):
        cps = copies(r)
        cps[0].wait_recv()
        to_up[r, :half] = (both(r, 1)[:half] + pass_in[r, :half].astype(f32)).astype(bf16)
        cps[4].start()
        cps[1].wait_recv()
        to_down[r, half:] = (both(r, 3)[half:] + pass_in[r, half:].astype(f32)).astype(bf16)
        cps[5].start()

    def finish(r):
        for cp in copies(r)[2:]:
            cp.wait_recv()
        swap(r, 0).wait_recv()
        out_ref[r * rc:(r + 1) * rc, :] = (
            both(r, 0) + from_down[r].astype(f32) + from_up[r].astype(f32)).astype(bf16)

    for i in range(OUT_CHUNKS + 5):
        if i < OUT_CHUNKS:
            share(i)
        if 1 <= i < OUT_CHUNKS + 1:
            leave(i - 1)
        if 3 <= i < OUT_CHUNKS + 3:
            add_on(i - 3)
        if i >= 5:
            finish(i - 5)
    drained()
    for r in range(OUT_CHUNKS):
        for j in range(4):
            swap(r, j).wait_send()
        for cp in copies(r):
            cp.wait_send()


def output(st, o, lift, z, nw, w):
    n = o.shape[0]
    rc = n // OUT_CHUNKS
    vm, anyw = pl.BlockSpec(memory_space=pltpu.VMEM), pl.BlockSpec(memory_space=pl.ANY)
    buf = pltpu.VMEM((OUT_CHUNKS, rc, 256), bf16)
    dma = pltpu.SemaphoreType.DMA
    return pl.pallas_call(
        output_kernel,
        in_specs=[vm, anyw, anyw, anyw, vm, anyw], out_specs=vm,
        out_shape=jax.ShapeDtypeStruct((n, 256), bf16),
        scratch_shapes=[
            pltpu.VMEM((n, 512), f32), pltpu.VMEM((n, 512), bf16), pltpu.VMEM((n, 512), bf16),
            pltpu.VMEM((512, 2048), bf16),
            pltpu.VMEM((4, HD, 2 * HD), bf16), pltpu.VMEM((4, HD, 2 * HD), bf16),
            pltpu.VMEM((HD, 2 * HD), bf16), pltpu.VMEM((HD, 2 * HD), bf16), pltpu.VMEM((HD, HD), bf16),
            pltpu.VMEM((4, HD, HD), bf16), pltpu.VMEM((4, HD, HD), bf16), pltpu.VMEM((OUT_CHUNKS, 4, rc, 256), f32),
            pltpu.VMEM((OUT_CHUNKS, 4, rc, 256), bf16), pltpu.VMEM((OUT_CHUNKS, 4, rc, 256), bf16),
            buf, buf, buf, buf, buf, buf,
            dma((4,)), dma((8,)), dma((8,)), dma((OUT_CHUNKS, 4)), dma((OUT_CHUNKS, 4)),
            dma((OUT_CHUNKS, 6)), dma((OUT_CHUNKS, 6))],
        compiler_params=pltpu.CompilerParams(collective_id=3, has_side_effects=True),
        name="output",
    )(st, o, lift, z, nw, w)


def per_device(hidden_in, w_query, w_key, w_value, w_gate, w_beta, w_alpha, dt_bias, head_decay,
               conv_query, conv_key, conv_value, norm_weight, w_out, prompt_lengths):
    o, lift, z, st = project(
        prompt_lengths, dt_bias, head_decay, hidden_in, w_query, w_key, w_value, w_gate, w_beta.T,
        w_alpha.T, conv_query, conv_key, conv_value)
    return output(st, o, lift, z, norm_weight[None, :], w_out)


def solution(mesh):
    rows, cols = P("seq", "head"), P(None, "head")
    in_specs = (rows, cols, cols, cols, cols, cols, cols, P("head"), P("head"), cols, cols, cols,
                P(), P("head", None), P())
    return jax.shard_map(per_device, mesh=mesh, in_specs=in_specs, out_specs=rows, check_vma=False)
```
